256 devices in a mesh: tm: 8 (over y_hi, x), cells: 32 (over z, y_lo, core).
Axes of the slice: x: 4, y: 4 (y_hi: 2, y_lo: 2; y = y_hi * 2 + y_lo), z: 8, core: 2. Of those that a mesh axis runs over, the one named last changes fastest.
Arguments:
- footprint: float32 [8, 4, 768, 8192], P('tm', None, None, 'cells'), may hold values from -0.03125 to 0.03125
- flux: float32 [8, 8192, 2048], P('tm', 'cells'), may hold values from -6 to 6
- obs_weight: float32 [8, 768], P('tm'), may hold values from 0.2 to 5
- obs_count: int32 [8], P('tm'), may hold values from 1 to 768, 4608 in all
Outputs:
- normal_image: float32 [8, 8192, 2048], P('tm', 'cells')
The draws below stay inside these ranges and needn't reach their ends.
Inputs may be any that keep to these rules, and one draw needn't show every extreme that they name: `obs_count`: each block has at least one valid slot; one block has all 768 slots valid.
All inputs are finite; a program needn't handle non-finite values.
Results may differ from the reference program's by a relative error of at most 0.0001.
Values sent between devices are 32-bit elements; how exact they have to be, the bound alone decides.
A program may use at most 128 MiB of HBM per device.

```python
import math
import jax
import jax.numpy as jnp
import numpy as np
from jax import lax

NC = 8192
NOBS = 768
LAGS = 4
K = 2048
NT = 8


def level_of(key, extent, split, least, high):
    level, own = 1.0, jax.random.fold_in(key, 6)
    for dim, parts in split:
        steps = jnp.exp(jax.random.uniform(jax.random.fold_in(own, dim), (parts,), jnp.float32, least / len(split), high / len(split)))
        level = level * jnp.repeat(steps, extent[dim] // parts).reshape([-1 if axis == dim else 1 for axis in range(len(extent))])
    return level


def profile(number_of, total, limit, skew):
    portions = [(1 << 20) // math.isqrt(rank ** skew) + 1 for rank in range(2, number_of + 1)]
    spare, counts = total - limit - (number_of - 1), [1] * (number_of - 1)
    while spare > 0:
        movable = [i for i in range(number_of - 1) if counts[i] < limit]
        whole, remaining = sum([portions[i] for i in movable]), spare
        for i in movable:
            extra = min(limit - counts[i], max(1, remaining * portions[i] // whole), spare)
            counts[i] = counts[i] + extra
            spare = spare - extra
    return np.array([limit] + counts)


def uneven(rng, amount, total, most, lean):
    if amount == 2:
        one = jax.random.randint(rng, (), max(1, total - most), min(most, total - 1) + 1)
        return jnp.stack([one, total - one])
    lengths = jnp.asarray(profile(amount, total, most, lean), jnp.int32)
    pairs = (amount - 1) // 2
    source_of, taker = lengths[1:1 + 2 * pairs:2], lengths[2:2 + 2 * pairs:2]
    margin = jnp.minimum(source_of - 1, most - taker)
    moved = jax.random.randint(jax.random.fold_in(rng, 1), (pairs,), 0, 1 << 20) % (margin + 1)
    lengths = lengths.at[1:1 + 2 * pairs:2].set(source_of - moved).at[2:2 + 2 * pairs:2].set(taker + moved)
    return lengths[jax.random.permutation(jax.random.fold_in(rng, 2), amount)]


def noise(rng, extent, scale, bound, shards=(), held_as=jnp.bfloat16):
    loudness = level_of(rng, extent, shards, -0.22, 0.18) if shards else 1.0
    drawn = jax.random.normal(rng, extent, jnp.float32) * scale * loudness
    return jnp.minimum(jnp.maximum(drawn, -bound), bound).astype(held_as)


def setup_inputs(seed: int = 0) -> dict:
    keys = jax.random.split(jax.random.key(seed), 5)
    footprint = noise(keys[0], (NT, LAGS, NOBS, NC), (LAGS * NC) ** -0.5, 0.03125, ((0, 8), (3, 32)), jnp.float32)
    flux = noise(keys[1], (NT, NC, K), 1.0, 6.0, ((0, 8), (1, 32)), jnp.float32)
    obs_weight = jnp.clip(jnp.exp(math.log(5.0) - 3.218876 * jax.random.uniform(keys[2], (NT, NOBS), jnp.float32) ** level_of(keys[2], (NT, NOBS), ((0, 8),), -0.2, 0.2)), 0.2, 5.0)
    obs_count = uneven(keys[3], NT, NT * NOBS * 3 // 4, NOBS, 0).astype(jnp.int32)
    return {"footprint": footprint, "flux": flux, "obs_weight": obs_weight, "obs_count": obs_count}


def reference(footprint, flux, obs_weight, obs_count):
    highest = lax.Precision.HIGHEST
    block_count = footprint.shape[0]
    lag_count = footprint.shape[1]
    slot_count = footprint.shape[2]
    valid = (jnp.arange(slot_count, dtype=jnp.int32)[None, :] < obs_count[:, None]).astype(jnp.float32)
    row_scale = valid * obs_weight
    weighted_list = []
    for tblock in range(block_count):
        modelled = jnp.zeros((slot_count, flux.shape[2]), jnp.float32)
        for lag_step in range(lag_count):
            if tblock - lag_step >= 0:
                modelled = modelled + jnp.dot(footprint[tblock, lag_step], flux[tblock - lag_step], precision=highest, preferred_element_type=jnp.float32)
        weighted_list.append(row_scale[tblock][:, None] * modelled)
    images = []
    for source in range(block_count):
        image = jnp.zeros((flux.shape[1], flux.shape[2]), jnp.float32)
        for lag_step in range(lag_count):
            if source + lag_step < block_count:
                image = image + lax.dot_general(footprint[source + lag_step, lag_step], weighted_list[source + lag_step], (((0,), (0,)), ((), ())), precision=highest, preferred_element_type=jnp.float32)
        images.append(image)
    return jnp.stack(images)
```

```python
import functools

import jax
import jax.numpy as jnp
from jax import lax
from jax.experimental import pallas as pl
from jax.experimental.pallas import tpu as pltpu
from jax.sharding import PartitionSpec as P

MESH = pl.DeviceIdType.MESH
CHUNKS = 8
LAGS = 4

S1, S3, R2, X2, X1, SA, SB, GB, GA, D2, D1, D3, E1, E2, SC = range(15)
H1, H2, H3 = S1, R2, S3


def split(value):
    high = value.astype(jnp.bfloat16)
    low = (value - high.astype(jnp.float32)).astype(jnp.bfloat16)
    return high, low


def kernel(
    foot, flux, scale, out,
    hal, part, got_a, got_b, got_c, full, adj, in1, in2, in3, in_a, in_b,
    h_hi, h_lo, t_hi, t_lo, f_hi, f_lo, w_hi, w_lo, send, recv,
):
    chunks, rows, width = part.shape
    deep = flux.shape[0]
    t = lax.axis_index("tm")
    place = lax.axis_index("cells")
    nz = lax.axis_size("cells") // 4
    tsize = lax.axis_size("tm")
    gz = nz - 1
    x = lax.rem(t, 4)
    z = place // 4
    y = lax.rem(place // 2, 2)
    core = lax.rem(place, 2)
    half, quarter, piece = rows // 2, rows // 4, rows // (4 * nz)
    other_core = z * 4 + y * 2 + (1 - core)
    other_y = z * 4 + (1 - y) * 2 + core

    def z_peer(step):
        return lax.rem(z + step, nz) * 4 + y * 2 + core

    def z_from(step):
        return lax.rem(z + nz - step, nz)

    barrier = pltpu.get_barrier_semaphore()
    for by in (1, 3, tsize - 1, tsize - 3):
        pl.semaphore_signal(barrier, inc=1, device_id=(lax.rem(t + by, tsize), place), device_id_type=MESH)
    for who in [other_core, other_y] + [z_peer(s) for s in range(1, nz)]:
        pl.semaphore_signal(barrier, inc=1, device_id=(t, who), device_id_type=MESH)
    pl.semaphore_wait(barrier, 4 + 2 + gz)

    def copy(src, dst, kind, c, to_t, to_place, into=None):
        into = kind if into is None else into
        return pltpu.make_async_remote_copy(
            src_ref=src, dst_ref=dst, send_sem=send.at[kind, c], recv_sem=recv.at[into, c],
            device_id=(to_t, to_place), device_id_type=MESH,
        )

    def cols(c):
        return pl.ds(pl.multiple_of(c * width, width), width)

    def own(c):
        return flux.at[:, cols(c)]

    def down(by):
        return lax.rem(t + by, tsize)

    def row(start, size):
        return pl.ds(pl.multiple_of(start, 8), size)

    mine_y = core * half + y * quarter
    theirs_y = core * half + (1 - y) * quarter
    mine_z = mine_y + z * piece

    cp = {
        S1: (x != 3, lambda c: copy(own(c), hal.at[0, c], S1, c, down(1), place)),
        S3: (t <= 4, lambda c: copy(own(c), hal.at[2, c], S3, c, down(3), place)),
        R2: ((x == 1) | (x == 2), lambda c: copy(hal.at[0, c], hal.at[1, c], R2, c, down(1), place)),
        X2: ((t == 5) | (t == 6), lambda c: copy(hal.at[2, c], hal.at[1, c], X2, c, down(tsize - 1), place, R2)),
        X1: (t == 5, lambda c: copy(hal.at[1, c], hal.at[0, c], X1, c, down(tsize - 1), place, S1)),
        SA: (None, lambda c: copy(part.at[c, row((1 - core) * half, half)], got_a.at[c], SA, c, t, other_core)),
        SB: (None, lambda c: copy(part.at[c, row(theirs_y, quarter)], got_b.at[c], SB, c, t, other_y)),
        GB: (None, lambda c: copy(full.at[c, row(mine_y, quarter)], full.at[c, row(mine_y, quarter)], GB, c, t, other_y)),
        GA: (None, lambda c: copy(full.at[c, row(core * half, half)], full.at[c, row(core * half, half)], GA, c, t, other_core)),
        D2: (x >= 2, lambda c: copy(adj.at[1, c], in2.at[c], D2, c, down(tsize - 1), place)),
        D1: (x >= 1, lambda c: copy(adj.at[0, c], in1.at[c], D1, c, down(tsize - 1), place)),
        D3: (t >= 3, lambda c: copy(adj.at[2, c], in3.at[c], D3, c, down(tsize - 3), place)),
        E1: ((t == 4) | (t == 5), lambda c: copy(adj.at[t - 4, c], in_a.at[c], E1, c, down(1), place)),
        E2: (t == 4, lambda c: copy(adj.at[1, c], in_b.at[c], E2, c, down(1), place)),
    }

    def c_send(step, c):
        to = lax.rem(z + step, nz)
        return copy(part.at[c, row(mine_y + to * piece, piece)], got_c.at[c, step - 1], SC + step - 1, c, t, z_peer(step))

    def c_gather(step, c):
        return copy(full.at[c, row(mine_z, piece)], full.at[c, row(mine_z, piece)], SC + gz + step - 1, c, t, z_peer(step))

    def start(kind, c, when=None):
        cond = cp[kind][0] if when is None else when
        if cond is None:
            cp[kind][1](c).start()
        else:
            pl.when(cond)(lambda: cp[kind][1](c).start())

    def landed(ref, kind, c, when=None):
        def wait():
            copy(ref, ref, kind, c, t, other_core).wait_recv()

        if when is None:
            wait()
        else:
            pl.when(when)(wait)

    relays_1 = (x == 1) | (x == 2)
    relays_3 = (t == 5) | (t == 6)

    def own_sends(c):
        start(S3, c)
        start(S1, c)

    def relay_1(c):
        landed(hal.at[0, c], H1, c, relays_1)
        start(R2, c)
        landed(hal.at[2, c], H3, c, relays_3)
        start(X2, c)

    def relay_2(c):
        landed(hal.at[1, c], H2, c, t == 5)
        start(X1, c)

    def forward(c):
        landed(hal.at[0, c], H1, c, (t >= 1) & ~relays_1)
        landed(hal.at[1, c], H2, c, (t >= 2) & (t != 5))
        landed(hal.at[2, c], H3, c, (t >= 3) & ~relays_3)
        for lag in range(LAGS):
            value = flux[:, cols(c)] if lag == 0 else hal[lag - 1, c]
            high, low = split(value)
            f_hi[lag * deep : (lag + 1) * deep, :] = high
            f_lo[lag * deep : (lag + 1) * deep, :] = low

        tile = rows // 4

        def block(m, carry):
            at = pl.ds(pl.multiple_of(m * tile, 8), tile)
            hh, hl = h_hi[at, :], h_lo[at, :]
            total = jnp.dot(hh, f_hi[...], preferred_element_type=jnp.float32)
            total = total + jnp.dot(hh, f_lo[...], preferred_element_type=jnp.float32)
            total = total + jnp.dot(hl, f_hi[...], preferred_element_type=jnp.float32)
            part[c, at, :] = total
            return carry

        lax.fori_loop(0, 4, block, 0)
        start(SA, c)

    def sum_a(c):
        landed(got_a.at[c], SA, c)
        at = row(core * half, half)
        part[c, at, :] = part[c, at, :] + got_a[c]
        start(SB, c)

    def sum_b(c):
        landed(got_b.at[c], SB, c)
        at = row(mine_y, quarter)
        part[c, at, :] = part[c, at, :] + got_b[c]
        for step in range(1, nz):
            c_send(step, c).start()

    def sum_c(c):
        total = part[c, row(mine_z, piece), :]
        for step in range(1, nz):
            landed(got_c.at[c, step - 1], SC + step - 1, c)
            total = total + got_c[c, step - 1]
        full[c, row(mine_z, piece), :] = total * scale[:, 0:1]
        for step in range(1, nz):
            c_gather(step, c).start()

    def gather_b(c):
        for step in range(1, nz):
            landed(full.at[c, row(mine_y + z_from(step) * piece, piece)], SC + gz + step - 1, c)
        start(GB, c)

    def gather_a(c):
        landed(full.at[c, row(theirs_y, quarter)], GB, c)
        start(GA, c)

    def adjoint(c):
        landed(full.at[c, row((1 - core) * half, half)], GA, c)
        high, low = split(full[c])
        w_hi[...] = high
        w_lo[...] = low

        def block(lag):
            at = pl.ds(lag * deep, deep)
            hh, hl = t_hi[at, :], t_lo[at, :]
            total = jnp.dot(hh, w_hi[...], preferred_element_type=jnp.float32)
            total = total + jnp.dot(hh, w_lo[...], preferred_element_type=jnp.float32)
            return total + jnp.dot(hl, w_hi[...], preferred_element_type=jnp.float32)

        adj[2, c] = block(3)
        adj[1, c] = block(2)
        start(D2, c)
        start(E2, c)
        start(D3, c, (t == 3) | (t == 4) | (t == 7))
        adj[0, c] = block(1)
        start(E1, c, t == 4)
        start(D1, c, x == 3)
        out[:, cols(c)] = block(0)

    def back_1(c):
        @pl.when(t == 5)
        def _():
            landed(in_a.at[c], E1, c)
            adj[1, c] = adj[1, c] + in_a[c]
            start(E1, c, t == 5)
            landed(in_b.at[c], E2, c)
            adj[2, c] = adj[2, c] + in_b[c]
            start(D3, c, t == 5)

        @pl.when(relays_1)
        def _():
            landed(in2.at[c], D2, c)
            adj[0, c] = adj[0, c] + in2[c]
            start(D1, c, x <= 2)

    def back_2(c):
        @pl.when(t == 6)
        def _():
            landed(in_a.at[c], E1, c)
            adj[2, c] = adj[2, c] + in_a[c]
            start(D3, c, t == 6)

    def finish(c):
        @pl.when(x <= 2)
        def _():
            landed(in1.at[c], D1, c)
            out[:, cols(c)] = out[:, cols(c)] + in1[c]

        @pl.when(t <= 4)
        def _():
            landed(in3.at[c], D3, c)
            out[:, cols(c)] = out[:, cols(c)] + in3[c]

    order = [
        (own_sends, -3),
        (relay_1, -2),
        (relay_2, -1),
        (forward, 0),
        (gather_a, 2),
        (sum_c, 1),
        (adjoint, 2),
        (sum_a, 0),
        (back_2, 3),
        (sum_b, 0),
        (gather_b, 1),
        (finish, 3),
        (back_1, 2),
    ]
    first, last = min(d for _, d in order), max(d for _, d in order)

    def step(i, carry):
        for stage, delay in order:
            c = i - delay
            pl.when((c >= 0) & (c < chunks))(functools.partial(stage, c))
        return carry

    def prepare(lag, carry):
        value = foot[lag]
        at = pl.ds(pl.multiple_of(lag * deep, deep), deep)
        h_hi[:, at], h_lo[:, at] = split(value)
        t_hi[at, :], t_lo[at, :] = split(value.T)
        return carry

    lead = 3
    for c in range(lead):
        own_sends(c)
    lax.fori_loop(0, LAGS, prepare, 0)
    for lag in range(1, LAGS):

        @pl.when(t < lag)
        def _(lag=lag):
            hal[lag - 1] = jnp.zeros(hal.shape[1:], hal.dtype)

    order[0] = (lambda c: pl.when(c >= lead)(functools.partial(own_sends, c)), order[0][1])
    lax.fori_loop(first, chunks + last, step, 0)

    def drain(c, carry):
        for kind, (cond, make) in cp.items():
            if cond is None:
                make(c).wait_send()
            else:
                pl.when(cond)(lambda make=make: make(c).wait_send())
        for s in range(1, nz):
            c_send(s, c).wait_send()
            c_gather(s, c).wait_send()
        return carry

    lax.fori_loop(0, chunks, drain, 0)


def on_device(footprint, flux, obs_weight, obs_count):
    lags, slots, deep = footprint.shape[1:]
    wide = flux.shape[2]
    chunks = CHUNKS
    width = wide // chunks
    nz = lax.axis_size("cells") // 4
    piece = slots // (4 * nz)
    place = lax.axis_index("cells")
    base = lax.rem(place, 2) * (slots // 2) + lax.rem(place // 2, 2) * (slots // 4) + (place // 4) * piece
    mine = base + jnp.arange(piece, dtype=jnp.int32)
    weight = lax.dynamic_slice(obs_weight[0], (base,), (piece,))
    row_scale = jnp.where(mine < obs_count[0], weight, 0.0)
    scale = jnp.broadcast_to(row_scale[:, None], (piece, 128))
    f32, bf16 = jnp.float32, jnp.bfloat16
    wide_block = pltpu.VMEM((chunks, deep, width), f32)
    kinds = SC + 2 * (nz - 1)
    result = pl.pallas_call(
        kernel,
        out_shape=jax.ShapeDtypeStruct((deep, wide), f32),
        in_specs=[pl.BlockSpec(memory_space=pltpu.VMEM)] * 3,
        out_specs=pl.BlockSpec(memory_space=pltpu.VMEM),
        scratch_shapes=[
            pltpu.VMEM((lags - 1, chunks, deep, width), f32),
            pltpu.VMEM((chunks, slots, width), f32),
            pltpu.VMEM((chunks, slots // 2, width), f32),
            pltpu.VMEM((chunks, slots // 4, width), f32),
            pltpu.VMEM((chunks, nz - 1, piece, width), f32),
            pltpu.VMEM((chunks, slots, width), f32),
            pltpu.VMEM((lags - 1, chunks, deep, width), f32),
            wide_block,
            wide_block,
            wide_block,
            wide_block,
            wide_block,
            pltpu.VMEM((slots, lags * deep), bf16),
            pltpu.VMEM((slots, lags * deep), bf16),
            pltpu.VMEM((lags * deep, slots), bf16),
            pltpu.VMEM((lags * deep, slots), bf16),
            pltpu.VMEM((lags * deep, width), bf16),
            pltpu.VMEM((lags * deep, width), bf16),
            pltpu.VMEM((slots, width), bf16),
            pltpu.VMEM((slots, width), bf16),
            pltpu.SemaphoreType.DMA((kinds, chunks)),
            pltpu.SemaphoreType.DMA((kinds, chunks)),
        ],
        compiler_params=pltpu.CompilerParams(
            collective_id=0, has_side_effects=True, vmem_limit_bytes=67043328
        ),
    )(footprint[0], flux[0], scale)
    return result[None]


def solution(mesh):
    placed = (P("tm", None, None, "cells"), P("tm", "cells", None), P("tm", None), P("tm"))
    return jax.shard_map(
        on_device, mesh=mesh, in_specs=placed, out_specs=P("tm", "cells", None), check_vma=False
    )
```

```python
import functools

import jax
import jax.numpy as jnp
from jax import lax
from jax.experimental import pallas as pl
from jax.experimental.pallas import tpu as pltpu
from jax.sharding import PartitionSpec as P

MESH = pl.DeviceIdType.MESH
CHUNKS = 8
LEAD = 2
ORDER = [("late_sends", -3), ("late_relay", -2), ("forward", 0), ("turn", 0), ("adjoint", 4), ("sum_3", 2), ("sum_2", 1), ("relay_2", -1), ("back_2", 5), ("sum_1", 0), ("gather_2", 3), ("finish", 7), ("gather_1", 2), ("back_1", 4), ("cross_1", 5)]
LAGS = 4

S1, S3, Y3, R2, X2, Z1, Z3, P0, P2, P4, SA, SB, TB, GB, HB, GA, D2, D1, D3, E1, E2, E3, F1, V3, W3, SC = range(26)
H1, H2, H3 = S1, R2, S3


def split(value):
    high = value.astype(jnp.bfloat16)
    low = (value - high.astype(jnp.float32)).astype(jnp.bfloat16)
    return high, low


def kernel(
    foot, flux, scale, out,
    hal, part, got_a, got_b, got_c, full, adj, in1, in2, in3, in_a, in_b,
    h_hi, h_lo, t_hi, t_lo, f_hi, f_lo, w_hi, w_lo, send, recv,
):
    chunks, rows, width = part.shape
    deep = flux.shape[0]
    t = lax.axis_index("tm")
    place = lax.axis_index("cells")
    nz = lax.axis_size("cells") // 4
    tsize = lax.axis_size("tm")
    gz = nz - 1
    x = lax.rem(t, 4)
    z = place // 4
    y = lax.rem(place // 2, 2)
    core = lax.rem(place, 2)
    half, quarter, piece = rows // 2, rows // 4, rows // (4 * nz)
    other_core = z * 4 + y * 2 + (1 - core)
    other_y = z * 4 + (1 - y) * 2 + core

    def z_peer(step):
        return lax.rem(z + step, nz) * 4 + y * 2 + core

    def z_from(step):
        return lax.rem(z + nz - step, nz)

    barrier = pltpu.get_barrier_semaphore()
    for by in (1, 3, 4, tsize - 1, tsize - 3):
        pl.semaphore_signal(barrier, inc=1, device_id=(lax.rem(t + by, tsize), place), device_id_type=MESH)
    for by in (1, 4, tsize - 1):
        pl.semaphore_signal(barrier, inc=1, device_id=(lax.rem(t + by, tsize), other_y), device_id_type=MESH)
    for who in [other_core, other_y] + [z_peer(s) for s in range(1, nz)]:
        pl.semaphore_signal(barrier, inc=1, device_id=(t, who), device_id_type=MESH)
    pl.semaphore_wait(barrier, 5 + 3 + 2 + gz)

    def copy(src, dst, kind, c, to_t, to_place, into=None):
        into = kind if into is None else into
        return pltpu.make_async_remote_copy(
            src_ref=src, dst_ref=dst, send_sem=send.at[kind, c], recv_sem=recv.at[into, c],
            device_id=(to_t, to_place), device_id_type=MESH,
        )

    def cols(c):
        return pl.ds(pl.multiple_of(c * width, width), width)

    def own(c):
        return flux.at[:, cols(c)]

    def down(by):
        return lax.rem(t + by, tsize)

    def row(start, size):
        return pl.ds(pl.multiple_of(start, 8), size)

    first = core == 0
    top = core * half
    pair = 2 * piece
    mine = jnp.where(first, top + y * quarter + z * piece, top + z * pair + y * piece)
    over_y = jnp.where(first, mine, top + z * pair + (1 - y) * piece)
    mine_y = top + y * quarter
    theirs_y = top + (1 - y) * quarter
    mine_z = top + z * pair
    sides = ((first, piece, mine_y), (~first, pair, top))

    relays_1 = (x == 1) | (x == 2)
    relays_3 = (t == 5) | (t == 6) | ((x == 3) & ~first)

    cp = {
        S1: (x != 3, lambda c: copy(own(c), hal.at[0, c], S1, c, down(1), place)),
        S3: ((t == 0) | ((t == 1) & first) | (t == 2) | (t == 4), lambda c: copy(own(c), hal.at[2, c], S3, c, down(3), place)),
        R2: (relays_1 & first, lambda c: copy(hal.at[0, c], hal.at[1, c], R2, c, down(1), place)),
        X2: (relays_3, lambda c: copy(hal.at[2, c], hal.at[1, c], X2, c, down(tsize - 1), place, R2)),
        Y3: (t == 3, lambda c: copy(own(c), in3.at[c], Y3, c, down(4), place)),
        P0: (((t == 1) | (t == 5)) & ~first, lambda c: copy(own(c), in2.at[c], P0, c, down(tsize - 1), place)),
        P2: ((x == 0) & ~first, lambda c: copy(in2.at[c], hal.at[1, c], P2, c, down(3), place, R2)),
        P4: ((t == 0) & ~first, lambda c: copy(in2.at[c], hal.at[2, c], P4, c, down(4), place, S3)),
        Z1: (t == 7, lambda c: copy(in3.at[c], hal.at[0, c], Z1, c, down(tsize - 3), place, S1)),
        Z3: (t == 7, lambda c: copy(in3.at[c], hal.at[2, c], Z3, c, down(tsize - 1), place, S3)),
        SA: (None, lambda c: copy(part.at[c, row((1 - core) * half, half)], got_a.at[c], SA, c, t, other_core)),
        SB: (first, lambda c: copy(part.at[c, row(theirs_y, quarter)], got_b.at[c], SB, c, t, other_y)),
        TB: (~first, lambda c: copy(part.at[c, row(over_y, piece)], got_b.at[c, 0:piece], TB, c, t, other_y, SB)),
        GB: (first, lambda c: copy(full.at[c, row(mine_y, quarter)], full.at[c, row(mine_y, quarter)], GB, c, t, other_y)),
        HB: (~first, lambda c: copy(full.at[c, row(mine, piece)], full.at[c, row(mine, piece)], HB, c, t, other_y, GB)),
        GA: (None, lambda c: copy(full.at[c, row(core * half, half)], full.at[c, row(core * half, half)], GA, c, t, other_core)),
        D2: (x >= 2, lambda c: copy(adj.at[1, c], in2.at[c], D2, c, down(tsize - 1), place)),
        D1: (x >= 1, lambda c: copy(adj.at[0, c], in1.at[c], D1, c, down(tsize - 1), place)),
        D3: (x == 3, lambda c: copy(adj.at[2, c], in3.at[c], D3, c, down(tsize - 3), place)),
        F1: (t == 7, lambda c: copy(in_a.at[c], in3.at[c], F1, c, down(tsize - 4), place, D3)),
        V3: ((t == 4) | (t == 5), lambda c: copy(adj.at[2, c], in_a.at[c], V3, c, down(tsize - 4), other_y)),
        W3: (t <= 1, lambda c: copy(in_a.at[c], in3.at[c], W3, c, down(1), other_y, D3)),
        E1: ((t == 5) | (t == 6), lambda c: copy(adj.at[t - 4, c], in_a.at[c], E1, c, down(1), place)),
        E2: (t == 4, lambda c: copy(adj.at[1, c], in_b.at[c], E2, c, down(1), place)),
        E3: (t == 4, lambda c: copy(adj.at[0, c], in_b.at[c], E3, c, down(3), place, E2)),
    }

    def c_send(step, c, size, base):
        to = lax.rem(z + step, nz)
        return copy(part.at[c, row(base + to * size, size)], got_c.at[c, step - 1, 0:size], SC + step - 1, c, t, z_peer(step))

    def c_gather(step, c, size, base):
        at = row(base + z * size, size)
        return copy(full.at[c, at], full.at[c, at], SC + gz + step - 1, c, t, z_peer(step))

    def start(kind, c, when=None):
        cond = cp[kind][0] if when is None else when
        if cond is None or cond is True:
            cp[kind][1](c).start()
        else:
            pl.when(cond)(lambda: cp[kind][1](c).start())

    def landed(ref, kind, c, when=None):
        def wait():
            copy(ref, ref, kind, c, t, other_core).wait_recv()

        if when is None:
            wait()
        else:
            pl.when(when)(wait)

    def own_sends(c):
        start(Y3, c)
        start(P0, c)
        start(S3, c)
        start(S1, c)

    def relay_1(c):
        @pl.when(t == 7)
        def _():
            landed(in3.at[c], Y3, c)
            start(Z1, c, True)
            start(Z3, c, True)

        @pl.when((x == 0) & ~first)
        def _():
            landed(in2.at[c], P0, c)
            start(P2, c, True)
            start(P4, c, t == 0)

        early = relays_3 & (t != 6)
        landed(hal.at[2, c], H3, c, early)
        start(X2, c, early)
        landed(hal.at[0, c], H1, c, relays_1 & first)
        start(R2, c)

    def relay_2(c):
        landed(hal.at[2, c], H3, c, t == 6)
        start(X2, c, t == 6)

    def forward(c):
        landed(hal.at[0, c], H1, c, (t >= 1) & ~(relays_1 & first))
        landed(hal.at[1, c], H2, c, t >= 2)
        landed(hal.at[2, c], H3, c, (t >= 3) & ~relays_3)
        for lag in range(LAGS):
            value = flux[:, cols(c)] if lag == 0 else hal[lag - 1, c]
            high, low = split(value)
            f_hi[lag * deep : (lag + 1) * deep, :] = high
            f_lo[lag * deep : (lag + 1) * deep, :] = low

        tile = rows // 4

        def block(m, carry):
            at = pl.ds(pl.multiple_of(m * tile, 8), tile)
            hh, hl = h_hi[at, :], h_lo[at, :]
            total = jnp.dot(hh, f_hi[...], preferred_element_type=jnp.float32)
            total = total + jnp.dot(hh, f_lo[...], preferred_element_type=jnp.float32)
            total = total + jnp.dot(hl, f_hi[...], preferred_element_type=jnp.float32)
            part[c, at, :] = total
            return carry

        lax.fori_loop(0, 4, block, 0)
        start(SA, c)

    def spread(c, size, base):
        for step in range(1, nz):
            c_send(step, c, size, base).start()

    def collect(c, size, base):
        at = row(base + z * size, size)
        total = part[c, at, :]
        for step in range(1, nz):
            landed(got_c.at[c, step - 1, 0:size], SC + step - 1, c)
            total = total + got_c[c, step - 1, 0:size, :]
        return at, total

    def share(c, size, base):
        for step in range(1, nz):
            c_gather(step, c, size, base).start()

    def shared(c, size, base):
        for step in range(1, nz):
            landed(full.at[c, row(base + z_from(step) * size, size)], SC + gz + step - 1, c)

    def sum_1(c):
        landed(got_a.at[c], SA, c)
        at = row(top, half)
        part[c, at, :] = part[c, at, :] + got_a[c]
        start(SB, c)
        pl.when(~first)(lambda: spread(c, pair, top))

    def sum_2(c):
        @pl.when(first)
        def _():
            landed(got_b.at[c], SB, c)
            at = row(mine_y, quarter)
            part[c, at, :] = part[c, at, :] + got_b[c]
            spread(c, piece, mine_y)

        @pl.when(~first)
        def _():
            at, total = collect(c, pair, top)
            part[c, at, :] = total
            start(TB, c, True)

    def sum_3(c):
        @pl.when(first)
        def _():
            at, total = collect(c, piece, mine_y)
            full[c, at, :] = total * scale[:, 0:1]
            share(c, piece, mine_y)

        @pl.when(~first)
        def _():
            landed(got_b.at[c, 0:piece], SB, c)
            at = row(mine, piece)
            full[c, at, :] = (part[c, at, :] + got_b[c, 0:piece]) * scale[:, 0:1]
            start(HB, c, True)

    def gather_1(c):
        @pl.when(first)
        def _():
            shared(c, piece, mine_y)
            start(GB, c, True)

        @pl.when(~first)
        def _():
            landed(full.at[c, row(over_y, piece)], GB, c)
            share(c, pair, top)

    def gather_2(c):
        landed(full.at[c, row(theirs_y, quarter)], GB, c, first)
        pl.when(~first)(lambda: shared(c, pair, top))
        start(GA, c)

    def adjoint(c):
        landed(full.at[c, row((1 - core) * half, half)], GA, c)
        high, low = split(full[c])
        w_hi[...] = high
        w_lo[...] = low

        def block(lag):
            at = pl.ds(lag * deep, deep)
            hh, hl = t_hi[at, :], t_lo[at, :]
            total = jnp.dot(hh, w_hi[...], preferred_element_type=jnp.float32)
            total = total + jnp.dot(hh, w_lo[...], preferred_element_type=jnp.float32)
            return total + jnp.dot(hl, w_hi[...], preferred_element_type=jnp.float32)

        adj[2, c] = block(3)
        adj[1, c] = block(2)
        start(D2, c)
        start(E2, c)
        start(E1, c, t == 5)
        start(D3, c)
        start(V3, c, t == 4)
        adj[0, c] = block(1)
        start(E3, c)
        start(D1, c, x == 3)
        out[:, cols(c)] = block(0)

    def back_1(c):
        @pl.when(t == 6)
        def _():
            landed(in_a.at[c], E1, c)
            adj[2, c] = adj[2, c] + in_a[c]
            start(E1, c, True)

        @pl.when(t == 5)
        def _():
            landed(in_b.at[c], E2, c)
            adj[2, c] = adj[2, c] + in_b[c]
            start(V3, c, True)

        @pl.when(relays_1)
        def _():
            landed(in2.at[c], D2, c)
            adj[0, c] = adj[0, c] + in2[c]
            start(D1, c, True)

    def back_2(c):
        @pl.when(t == 7)
        def _():
            landed(in_b.at[c], E2, c)
            landed(in_a.at[c], E1, c)
            in_a[c] = in_a[c] + in_b[c]
            start(F1, c, True)

    def cross_1(c):
        landed(in_a.at[c], V3, c, t <= 1)
        start(W3, c)

    def finish(c):
        @pl.when(x <= 2)
        def _():
            landed(in1.at[c], D1, c)
            out[:, cols(c)] = out[:, cols(c)] + in1[c]

        @pl.when(t <= 4)
        def _():
            landed(in3.at[c], D3, c)
            out[:, cols(c)] = out[:, cols(c)] + in3[c]

    def split_rows(lag):
        at = pl.ds(lag * deep, deep)
        h_hi[:, at], h_lo[:, at] = split(foot[lag])

    def split_turned(lag):
        at = pl.ds(lag * deep, deep)
        t_hi[at, :], t_lo[at, :] = split(foot[lag].T)

    def late_sends(c):
        pl.when(c >= LEAD)(lambda: own_sends(c))

    for c in range(LEAD):
        own_sends(c)
    split_rows(0)
    split_rows(1)
    relay_1(0)
    split_rows(2)
    split_rows(3)
    for lag in range(1, LAGS):

        @pl.when(t < lag)
        def _(lag=lag):
            hal[lag - 1] = jnp.zeros(hal.shape[1:], hal.dtype)

    def late_relay(c):
        pl.when(c >= 1)(lambda: relay_1(c))

    def turn(c):
        @pl.when(c == 0)
        def _():
            for lag in range(LAGS):
                split_turned(lag)

    named = locals()
    order = [(named[name], delay) for name, delay in ORDER]
    begin, end = min(d for _, d in order), max(d for _, d in order)

    def step(i, carry):
        for stage, delay in order:
            c = i - delay
            @pl.when((c >= 0) & (c < chunks))
            def _(stage=stage, c=c):
                with jax.named_scope(stage.__name__):
                    stage(c)
        return carry

    lax.fori_loop(begin, chunks + end, step, 0)

    def drain(c, carry):
        for kind, (cond, make) in cp.items():
            if cond is None:
                make(c).wait_send()
            else:
                pl.when(cond)(lambda make=make: make(c).wait_send())
        for cond, size, base in sides:

            @pl.when(cond)
            def _(size=size, base=base):
                for s in range(1, nz):
                    c_send(s, c, size, base).wait_send()
                    c_gather(s, c, size, base).wait_send()

        return carry

    lax.fori_loop(0, chunks, drain, 0)


def on_device(footprint, flux, obs_weight, obs_count):
    lags, slots, deep = footprint.shape[1:]
    wide = flux.shape[2]
    chunks = CHUNKS
    width = wide // chunks
    nz = lax.axis_size("cells") // 4
    piece = slots // (4 * nz)
    place = lax.axis_index("cells")
    core, y, z = lax.rem(place, 2), lax.rem(place // 2, 2), place // 4
    inner = jnp.where(core == 0, y * (slots // 4) + z * piece, (2 * z + y) * piece)
    base = core * (slots // 2) + inner
    mine = base + jnp.arange(piece, dtype=jnp.int32)
    weight = lax.dynamic_slice(obs_weight[0], (base,), (piece,))
    row_scale = jnp.where(mine < obs_count[0], weight, 0.0)
    scale = jnp.broadcast_to(row_scale[:, None], (piece, 128))
    f32, bf16 = jnp.float32, jnp.bfloat16
    wide_block = pltpu.VMEM((chunks, deep, width), f32)
    kinds = SC + 2 * (nz - 1)
    result = pl.pallas_call(
        kernel,
        out_shape=jax.ShapeDtypeStruct((deep, wide), f32),
        in_specs=[pl.BlockSpec(memory_space=pltpu.VMEM)] * 3,
        out_specs=pl.BlockSpec(memory_space=pltpu.VMEM),
        scratch_shapes=[
            pltpu.VMEM((lags - 1, chunks, deep, width), f32),
            pltpu.VMEM((chunks, slots, width), f32),
            pltpu.VMEM((chunks, slots // 2, width), f32),
            pltpu.VMEM((chunks, slots // 4, width), f32),
            pltpu.VMEM((chunks, nz - 1, 2 * piece, width), f32),
            pltpu.VMEM((chunks, slots, width), f32),
            pltpu.VMEM((lags - 1, chunks, deep, width), f32),
            wide_block,
            wide_block,
            wide_block,
            wide_block,
            wide_block,
            pltpu.VMEM((slots, lags * deep), bf16),
            pltpu.VMEM((slots, lags * deep), bf16),
            pltpu.VMEM((lags * deep, slots), bf16),
            pltpu.VMEM((lags * deep, slots), bf16),
            pltpu.VMEM((lags * deep, width), bf16),
            pltpu.VMEM((lags * deep, width), bf16),
            pltpu.VMEM((slots, width), bf16),
            pltpu.VMEM((slots, width), bf16),
            pltpu.SemaphoreType.DMA((kinds, chunks)),
            pltpu.SemaphoreType.DMA((kinds, chunks)),
        ],
        compiler_params=pltpu.CompilerParams(
            collective_id=0, has_side_effects=True, vmem_limit_bytes=67043328
        ),
    )(footprint[0], flux[0], scale)
    return result[None]


def solution(mesh):
    placed = (P("tm", None, None, "cells"), P("tm", "cells", None), P("tm", None), P("tm"))
    return jax.shard_map(
        on_device, mesh=mesh, in_specs=placed, out_specs=P("tm", "cells", None), check_vma=False
    )
```

```python
import functools

import jax
import jax.numpy as jnp
from jax import lax
from jax.experimental import pallas as pl
from jax.experimental.pallas import tpu as pltpu
from jax.sharding import PartitionSpec as P

MESH = pl.DeviceIdType.MESH
CHUNKS = 8
LEAD = 2
ORDER = [("late_sends", -3), ("late_relay", -2), ("forward", 0), ("turn", 0), ("gather_1", 3), ("adjoint", 4), ("sum_3", 2), ("sum_2", 1), ("relay_2", -1), ("back_2", 6), ("sum_1", 0), ("gather_2", 3), ("finish", 8), ("back_1", 5), ("cross_1", 6)]
LAGS = 4

S1, S3, Y3, R2, X2, Z1, Z3, P0, P2, P4, SA, SB, TB, GB, HB, GA, D2, D1, D3, E1, E2, E3, F1, V3, W3, G2, G3, V1, W1, U1, SC = range(31)
H1, H2, H3 = S1, R2, S3


def split(value):
    high = value.astype(jnp.bfloat16)
    low = (value - high.astype(jnp.float32)).astype(jnp.bfloat16)
    return high, low


def kernel(
    foot, flux, scale, out,
    hal, part, got_a, got_b, got_c, full, adj, in1, in2, in3, in_a, in_b,
    h_hi, h_lo, t_hi, t_lo, f_hi, f_lo, w_hi, w_lo, send, recv,
):
    chunks, rows, width = part.shape
    deep = flux.shape[0]
    t = lax.axis_index("tm")
    place = lax.axis_index("cells")
    nz = lax.axis_size("cells") // 4
    tsize = lax.axis_size("tm")
    gz = nz - 1
    x = lax.rem(t, 4)
    z = place // 4
    y = lax.rem(place // 2, 2)
    core = lax.rem(place, 2)
    half, quarter, piece = rows // 2, rows // 4, rows // (4 * nz)
    other_core = z * 4 + y * 2 + (1 - core)
    other_y = z * 4 + (1 - y) * 2 + core

    def z_peer(step):
        return lax.rem(z + step, nz) * 4 + y * 2 + core

    def z_from(step):
        return lax.rem(z + nz - step, nz)

    barrier = pltpu.get_barrier_semaphore()
    for by in (1, 3, 4, tsize - 1, tsize - 3):
        pl.semaphore_signal(barrier, inc=1, device_id=(lax.rem(t + by, tsize), place), device_id_type=MESH)
    for by in (1, 4, tsize - 1):
        pl.semaphore_signal(barrier, inc=1, device_id=(lax.rem(t + by, tsize), other_y), device_id_type=MESH)
    for who in [other_core, other_y] + [z_peer(s) for s in range(1, nz)]:
        pl.semaphore_signal(barrier, inc=1, device_id=(t, who), device_id_type=MESH)
    with jax.named_scope('p_barrier'):
        pl.semaphore_wait(barrier, 5 + 3 + 2 + gz)

    def copy(src, dst, kind, c, to_t, to_place, into=None):
        into = kind if into is None else into
        return pltpu.make_async_remote_copy(
            src_ref=src, dst_ref=dst, send_sem=send.at[kind, c], recv_sem=recv.at[into, c],
            device_id=(to_t, to_place), device_id_type=MESH,
        )

    def cols(c):
        return pl.ds(pl.multiple_of(c * width, width), width)

    def own(c):
        return flux.at[:, cols(c)]

    def down(by):
        return lax.rem(t + by, tsize)

    def row(start, size):
        return pl.ds(pl.multiple_of(start, 8), size)

    first = core == 0
    y_first = core == 0
    top = core * half
    pair = 2 * piece
    mine = jnp.where(y_first, top + y * quarter + z * piece, top + z * pair + y * piece)
    over_y = jnp.where(y_first, mine, top + z * pair + (1 - y) * piece)
    mine_y = top + y * quarter
    theirs_y = top + (1 - y) * quarter
    mine_z = top + z * pair
    sides = ((y_first, piece, mine_y), (~y_first, pair, top))

    relays_1 = (x == 1) | (x == 2)
    relays_3 = (t == 5) | (t == 6) | ((x == 3) & ~first)

    cp = {
        S1: (x != 3, lambda c: copy(own(c), hal.at[0, c], S1, c, down(1), place)),
        S3: ((t == 0) | ((t == 1) & first) | (t == 2) | (t == 4), lambda c: copy(own(c), hal.at[2, c], S3, c, down(3), place)),
        R2: (relays_1 & first, lambda c: copy(hal.at[0, c], hal.at[1, c], R2, c, down(1), place)),
        X2: (relays_3, lambda c: copy(hal.at[2, c], hal.at[1, c], X2, c, down(tsize - 1), place, R2)),
        Y3: (t == 3, lambda c: copy(own(c), in3.at[c], Y3, c, down(4), place)),
        P0: (((t == 1) | (t == 5)) & ~first, lambda c: copy(own(c), in2.at[c], P0, c, down(tsize - 1), place)),
        P2: ((x == 0) & ~first, lambda c: copy(in2.at[c], hal.at[1, c], P2, c, down(3), place, R2)),
        P4: ((t == 0) & ~first, lambda c: copy(in2.at[c], hal.at[2, c], P4, c, down(4), place, S3)),
        Z1: (t == 7, lambda c: copy(in3.at[c], hal.at[0, c], Z1, c, down(tsize - 3), place, S1)),
        Z3: (t == 7, lambda c: copy(in3.at[c], hal.at[2, c], Z3, c, down(tsize - 1), place, S3)),
        SA: (None, lambda c: copy(part.at[c, row((1 - core) * half, half)], got_a.at[c], SA, c, t, other_core)),
        SB: (y_first, lambda c: copy(part.at[c, row(theirs_y, quarter)], got_b.at[c], SB, c, t, other_y)),
        TB: (~y_first, lambda c: copy(part.at[c, row(over_y, piece)], got_b.at[c, 0:piece], TB, c, t, other_y, SB)),
        GB: (y_first, lambda c: copy(full.at[c, row(mine_y, quarter)], full.at[c, row(mine_y, quarter)], GB, c, t, other_y)),
        HB: (~y_first, lambda c: copy(full.at[c, row(mine, piece)], full.at[c, row(mine, piece)], HB, c, t, other_y, GB)),
        GA: (None, lambda c: copy(full.at[c, row(core * half, half)], full.at[c, row(core * half, half)], GA, c, t, other_core)),
        D2: ((x >= 2) & first, lambda c: copy(adj.at[1, c], in2.at[c], D2, c, down(tsize - 1), place)),
        D1: (x >= 1, lambda c: copy(adj.at[0, c], in1.at[c], D1, c, down(tsize - 1), place)),
        D3: (x == 3, lambda c: copy(adj.at[2, c], in3.at[c], D3, c, down(tsize - 3), place)),
        F1: (t == 7, lambda c: copy(in_a.at[c], in3.at[c], F1, c, down(tsize - 4), place, D3)),
        V3: (((t == 4) & first) | (t == 5), lambda c: copy(adj.at[2, c], in_a.at[c], V3, c, down(tsize - 4), other_y)),
        G2: ((x == 2) & ~first, lambda c: copy(adj.at[1, c], in2.at[c], G2, c, down(1), place, D2)),
        G3: ((x == 3) & ~first, lambda c: copy(adj.at[1, c], in_b.at[c], G3, c, down(tsize - 3), place, E2)),
        V1: ((t == 4) & ~first, lambda c: copy(adj.at[2, c], in_a.at[c], V1, c, down(tsize - 4), place, V3)),
        W1: ((t == 0) & ~first, lambda c: copy(in_a.at[c], in3.at[c], W1, c, down(1), place, D3)),
        U1: ((t == 4) & ~first, lambda c: copy(in_b.at[c], in3.at[c], U1, c, down(1), place, D3)),
        W3: (((t == 0) & first) | (t == 1), lambda c: copy(in_a.at[c], in3.at[c], W3, c, down(1), other_y, D3)),
        E1: ((t == 5) | (t == 6), lambda c: copy(adj.at[t - 4, c], in_a.at[c], E1, c, down(1), place)),
        E2: (t == 4, lambda c: copy(adj.at[1, c], in_b.at[c], E2, c, down(1), place)),
        E3: (t == 4, lambda c: copy(adj.at[0, c], in_b.at[c], E3, c, down(3), place, E2)),
    }

    def c_send(step, c, size, base):
        to = lax.rem(z + step, nz)
        return copy(part.at[c, row(base + to * size, size)], got_c.at[c, step - 1, 0:size], SC + step - 1, c, t, z_peer(step))

    def c_gather(step, c, size, base):
        at = row(base + z * size, size)
        return copy(full.at[c, at], full.at[c, at], SC + gz + step - 1, c, t, z_peer(step))

    def start(kind, c, when=None):
        cond = cp[kind][0] if when is None else when
        if cond is None or cond is True:
            cp[kind][1](c).start()
        else:
            pl.when(cond)(lambda: cp[kind][1](c).start())

    def landed(ref, kind, c, when=None):
        def wait():
            copy(ref, ref, kind, c, t, other_core).wait_recv()

        if when is None:
            wait()
        else:
            pl.when(when)(wait)

    def own_sends(c):
        start(Y3, c)
        start(P0, c)
        start(S3, c)
        start(S1, c)

    def relay_1(c):
        @pl.when(t == 7)
        def _():
            landed(in3.at[c], Y3, c)
            start(Z1, c, True)
            start(Z3, c, True)

        @pl.when((x == 0) & ~first)
        def _():
            landed(in2.at[c], P0, c)
            start(P2, c, True)
            start(P4, c, t == 0)

        early = relays_3 & (t != 6)
        landed(hal.at[2, c], H3, c, early)
        start(X2, c, early)
        landed(hal.at[0, c], H1, c, relays_1 & first)
        start(R2, c)

    def relay_2(c):
        landed(hal.at[2, c], H3, c, t == 6)
        start(X2, c, t == 6)

    def forward(c):
        landed(hal.at[0, c], H1, c, (t >= 1) & ~(relays_1 & first))
        landed(hal.at[1, c], H2, c, t >= 2)
        landed(hal.at[2, c], H3, c, (t >= 3) & ~relays_3)
        for lag in range(LAGS):
            value = flux[:, cols(c)] if lag == 0 else hal[lag - 1, c]
            high, low = split(value)
            f_hi[lag * deep : (lag + 1) * deep, :] = high
            f_lo[lag * deep : (lag + 1) * deep, :] = low

        tile = rows // 4

        def block(m, carry):
            at = pl.ds(pl.multiple_of(m * tile, 8), tile)
            hh, hl = h_hi[at, :], h_lo[at, :]
            total = jnp.dot(hh, f_hi[...], preferred_element_type=jnp.float32)
            total = total + jnp.dot(hh, f_lo[...], preferred_element_type=jnp.float32)
            total = total + jnp.dot(hl, f_hi[...], preferred_element_type=jnp.float32)
            part[c, at, :] = total
            return carry

        lax.fori_loop(0, 4, block, 0)
        start(SA, c)

    def spread(c, size, base):
        for step in range(1, nz):
            c_send(step, c, size, base).start()

    def collect(c, size, base):
        at = row(base + z * size, size)
        total = part[c, at, :]
        for step in range(1, nz):
            landed(got_c.at[c, step - 1, 0:size], SC + step - 1, c)
            total = total + got_c[c, step - 1, 0:size, :]
        return at, total

    def share(c, size, base):
        for step in range(1, nz):
            c_gather(step, c, size, base).start()

    def shared(c, size, base):
        for step in range(1, nz):
            landed(full.at[c, row(base + z_from(step) * size, size)], SC + gz + step - 1, c)

    def sum_1(c):
        landed(got_a.at[c], SA, c)
        at = row(top, half)
        part[c, at, :] = part[c, at, :] + got_a[c]
        start(SB, c)
        pl.when(~y_first)(lambda: spread(c, pair, top))

    def sum_2(c):
        @pl.when(y_first)
        def _():
            landed(got_b.at[c], SB, c)
            at = row(mine_y, quarter)
            part[c, at, :] = part[c, at, :] + got_b[c]
            spread(c, piece, mine_y)

        @pl.when(~y_first)
        def _():
            at, total = collect(c, pair, top)
            part[c, at, :] = total
            start(TB, c, True)

    def sum_3(c):
        @pl.when(y_first)
        def _():
            at, total = collect(c, piece, mine_y)
            full[c, at, :] = total * scale[:, 0:1]
            share(c, piece, mine_y)

        @pl.when(~y_first)
        def _():
            landed(got_b.at[c, 0:piece], SB, c)
            at = row(mine, piece)
            full[c, at, :] = (part[c, at, :] + got_b[c, 0:piece]) * scale[:, 0:1]
            start(HB, c, True)

    def gather_1(c):
        @pl.when(y_first)
        def _():
            shared(c, piece, mine_y)
            start(GB, c, True)

        @pl.when(~y_first)
        def _():
            landed(full.at[c, row(over_y, piece)], GB, c)
            share(c, pair, top)

    def gather_2(c):
        landed(full.at[c, row(theirs_y, quarter)], GB, c, y_first)
        pl.when(~y_first)(lambda: shared(c, pair, top))
        start(GA, c)

    def adjoint(c):
        landed(full.at[c, row((1 - core) * half, half)], GA, c)
        high, low = split(full[c])
        w_hi[...] = high
        w_lo[...] = low

        def block(lag):
            at = pl.ds(lag * deep, deep)
            hh, hl = t_hi[at, :], t_lo[at, :]
            total = jnp.dot(hh, w_hi[...], preferred_element_type=jnp.float32)
            total = total + jnp.dot(hh, w_lo[...], preferred_element_type=jnp.float32)
            return total + jnp.dot(hl, w_hi[...], preferred_element_type=jnp.float32)

        adj[2, c] = block(3)
        adj[1, c] = block(2)
        start(D2, c)
        start(G2, c)
        start(G3, c)
        start(E2, c)
        start(E1, c, t == 5)
        start(D3, c, (x == 3) & first)
        start(V3, c, (t == 4) & first)
        start(V1, c)
        adj[0, c] = block(1)
        start(E3, c)
        start(D1, c, (x == 3) | ((x >= 1) & ~first))
        out[:, cols(c)] = block(0)

    def back_1(c):
        @pl.when(t == 6)
        def _():
            landed(in_a.at[c], E1, c)
            adj[2, c] = adj[2, c] + in_a[c]
            start(E1, c, True)

        @pl.when(t == 5)
        def _():
            landed(in_b.at[c], E2, c)
            adj[2, c] = adj[2, c] + in_b[c]
            start(V3, c, True)

        @pl.when(relays_1 & first)
        def _():
            landed(in2.at[c], D2, c)
            adj[0, c] = adj[0, c] + in2[c]
            start(D1, c, True)

        @pl.when((x == 3) & ~first)
        def _():
            landed(in2.at[c], D2, c)
            adj[2, c] = adj[2, c] + in2[c]
            start(D3, c, True)

        @pl.when((t == 0) & ~first)
        def _():
            landed(in_a.at[c], V3, c)
            landed(in_b.at[c], E2, c)
            in_a[c] = in_a[c] + in_b[c]
            start(W1, c, True)

        @pl.when((t == 4) & ~first)
        def _():
            landed(in_b.at[c], E2, c)
            start(U1, c, True)

    def back_2(c):
        @pl.when(t == 7)
        def _():
            landed(in_b.at[c], E2, c)
            landed(in_a.at[c], E1, c)
            in_a[c] = in_a[c] + in_b[c]
            start(F1, c, True)

    def cross_1(c):
        landed(in_a.at[c], V3, c, cp[W3][0])
        start(W3, c)

    def finish(c):
        @pl.when(x <= 2)
        def _():
            landed(in1.at[c], D1, c)
            out[:, cols(c)] = out[:, cols(c)] + in1[c]

        @pl.when((t <= 4) | ((t == 5) & ~first))
        def _():
            landed(in3.at[c], D3, c)
            out[:, cols(c)] = out[:, cols(c)] + in3[c]

    def split_rows(lag):
        at = pl.ds(lag * deep, deep)
        h_hi[:, at], h_lo[:, at] = split(foot[lag])

    def split_turned(lag):
        at = pl.ds(lag * deep, deep)
        t_hi[at, :], t_lo[at, :] = split(foot[lag].T)

    def late_sends(c):
        pl.when(c >= LEAD)(lambda: own_sends(c))

    for c in range(LEAD):
        own_sends(c)
    with jax.named_scope('p_split'):
        split_rows(0)
        split_rows(1)
    with jax.named_scope('p_relay'):
        relay_1(0)
    with jax.named_scope('p_split'):
        split_rows(2)
        split_rows(3)
    for lag in range(1, LAGS):

        @pl.when(t < lag)
        def _(lag=lag):
            hal[lag - 1] = jnp.zeros(hal.shape[1:], hal.dtype)

    def late_relay(c):
        pl.when(c >= 1)(lambda: relay_1(c))

    def turn(c):
        @pl.when(c == 0)
        def _():
            for lag in range(LAGS):
                split_turned(lag)

    named = locals()
    order = [(named[name], delay) for name, delay in ORDER]
    begin, end = min(d for _, d in order), max(d for _, d in order)

    def step(i, carry):
        for stage, delay in order:
            c = i - delay
            @pl.when((c >= 0) & (c < chunks))
            def _(stage=stage, c=c):
                with jax.named_scope(stage.__name__):
                    stage(c)
        return carry

    lax.fori_loop(begin, chunks + end, step, 0)

    def drain(c, carry):
        for kind, (cond, make) in cp.items():
            if cond is None:
                make(c).wait_send()
            else:
                pl.when(cond)(lambda make=make: make(c).wait_send())
        for cond, size, base in sides:

            @pl.when(cond)
            def _(size=size, base=base):
                for s in range(1, nz):
                    c_send(s, c, size, base).wait_send()
                    c_gather(s, c, size, base).wait_send()

        return carry

    lax.fori_loop(0, chunks, drain, 0)


def on_device(footprint, flux, obs_weight, obs_count):
    lags, slots, deep = footprint.shape[1:]
    wide = flux.shape[2]
    chunks = CHUNKS
    width = wide // chunks
    nz = lax.axis_size("cells") // 4
    piece = slots // (4 * nz)
    place = lax.axis_index("cells")
    core, y, z = lax.rem(place, 2), lax.rem(place // 2, 2), place // 4
    inner = jnp.where(core == 0, y * (slots // 4) + z * piece, (2 * z + y) * piece)
    base = core * (slots // 2) + inner
    mine = base + jnp.arange(piece, dtype=jnp.int32)
    weight = lax.dynamic_slice(obs_weight[0], (base,), (piece,))
    row_scale = jnp.where(mine < obs_count[0], weight, 0.0)
    scale = jnp.broadcast_to(row_scale[:, None], (piece, 128))
    f32, bf16 = jnp.float32, jnp.bfloat16
    wide_block = pltpu.VMEM((chunks, deep, width), f32)
    kinds = SC + 2 * (nz - 1)
    result = pl.pallas_call(
        kernel,
        out_shape=jax.ShapeDtypeStruct((deep, wide), f32),
        in_specs=[pl.BlockSpec(memory_space=pltpu.VMEM)] * 3,
        out_specs=pl.BlockSpec(memory_space=pltpu.VMEM),
        scratch_shapes=[
            pltpu.VMEM((lags - 1, chunks, deep, width), f32),
            pltpu.VMEM((chunks, slots, width), f32),
            pltpu.VMEM((chunks, slots // 2, width), f32),
            pltpu.VMEM((chunks, slots // 4, width), f32),
            pltpu.VMEM((chunks, nz - 1, 2 * piece, width), f32),
            pltpu.VMEM((chunks, slots, width), f32),
            pltpu.VMEM((lags - 1, chunks, deep, width), f32),
            wide_block,
            wide_block,
            wide_block,
            wide_block,
            wide_block,
            pltpu.VMEM((slots, lags * deep), bf16),
            pltpu.VMEM((slots, lags * deep), bf16),
            pltpu.VMEM((lags * deep, slots), bf16),
            pltpu.VMEM((lags * deep, slots), bf16),
            pltpu.VMEM((lags * deep, width), bf16),
            pltpu.VMEM((lags * deep, width), bf16),
            pltpu.VMEM((slots, width), bf16),
            pltpu.VMEM((slots, width), bf16),
            pltpu.SemaphoreType.DMA((kinds, chunks)),
            pltpu.SemaphoreType.DMA((kinds, chunks)),
        ],
        compiler_params=pltpu.CompilerParams(
            collective_id=0, has_side_effects=True, vmem_limit_bytes=67043328
        ),
    )(footprint[0], flux[0], scale)
    return result[None]


def solution(mesh):
    placed = (P("tm", None, None, "cells"), P("tm", "cells", None), P("tm", None), P("tm"))
    return jax.shard_map(
        on_device, mesh=mesh, in_specs=placed, out_specs=P("tm", "cells", None), check_vma=False
    )
```

```python
import functools

import jax
import jax.numpy as jnp
from jax import lax
from jax.experimental import pallas as pl
from jax.experimental.pallas import tpu as pltpu
from jax.sharding import PartitionSpec as P

MESH = pl.DeviceIdType.MESH
CHUNKS = 8
LEAD = 2
ORDER = [("late_sends", -2), ("late_relay", -2), ("forward", 0), ("turn", 0), ("gather_1", 3), ("adjoint", 4), ("sum_3", 2), ("sum_2", 1), ("relay_2", -1), ("back_2", 6), ("sum_1", 0), ("gather_2", 3), ("finish", 8), ("back_1", 5), ("cross_1", 6)]
LAGS = 4

S1, S3, Y3, R2, X2, Z1, Z3, P0, P2, P4, SA, SB, TB, GB, HB, GA, D2, D1, D3, E1, E2, E3, F1, V3, W3, G2, G3, V1, W1, U1, SC = range(31)
H1, H2, H3 = S1, R2, S3


def split(value):
    high = value.astype(jnp.bfloat16)
    low = (value - high.astype(jnp.float32)).astype(jnp.bfloat16)
    return high, low


def kernel(
    foot, flux, scale, out,
    hal, part, got_a, got_b, got_c, full, adj, in1, in2, in3, in_a, in_b,
    h_hi, h_lo, t_hi, t_lo, f_hi, f_lo, w_hi, w_lo, send, recv,
):
    chunks, rows, width = part.shape
    deep = flux.shape[0]
    t = lax.axis_index("tm")
    place = lax.axis_index("cells")
    nz = lax.axis_size("cells") // 4
    tsize = lax.axis_size("tm")
    gz = nz - 1
    x = lax.rem(t, 4)
    z = place // 4
    y = lax.rem(place // 2, 2)
    core = lax.rem(place, 2)
    half, quarter, piece = rows // 2, rows // 4, rows // (4 * nz)
    other_core = z * 4 + y * 2 + (1 - core)
    other_y = z * 4 + (1 - y) * 2 + core

    def z_peer(step):
        return lax.rem(z + step, nz) * 4 + y * 2 + core

    def z_from(step):
        return lax.rem(z + nz - step, nz)

    barrier = pltpu.get_barrier_semaphore()
    for by in (1, 3, 4, tsize - 1, tsize - 3):
        pl.semaphore_signal(barrier, inc=1, device_id=(lax.rem(t + by, tsize), place), device_id_type=MESH)
    for by in (1, 4, tsize - 1):
        pl.semaphore_signal(barrier, inc=1, device_id=(lax.rem(t + by, tsize), other_y), device_id_type=MESH)
    for who in [other_core, other_y] + [z_peer(s) for s in range(1, nz)]:
        pl.semaphore_signal(barrier, inc=1, device_id=(t, who), device_id_type=MESH)
    with jax.named_scope('p_barrier'):
        pl.semaphore_wait(barrier, 5 + 3 + 2 + gz)

    def copy(src, dst, kind, c, to_t, to_place, into=None):
        into = kind if into is None else into
        return pltpu.make_async_remote_copy(
            src_ref=src, dst_ref=dst, send_sem=send.at[kind, c], recv_sem=recv.at[into, c],
            device_id=(to_t, to_place), device_id_type=MESH,
        )

    def cols(c):
        return pl.ds(pl.multiple_of(c * width, width), width)

    def own(c):
        return flux.at[:, cols(c)]

    def down(by):
        return lax.rem(t + by, tsize)

    def row(start, size):
        return pl.ds(pl.multiple_of(start, 8), size)

    first = core == 0
    y_first = core == 0
    top = core * half
    pair = 2 * piece
    mine = jnp.where(y_first, top + y * quarter + z * piece, top + z * pair + y * piece)
    over_y = jnp.where(y_first, mine, top + z * pair + (1 - y) * piece)
    mine_y = top + y * quarter
    theirs_y = top + (1 - y) * quarter
    mine_z = top + z * pair
    sides = ((y_first, piece, mine_y), (~y_first, pair, top))

    relays_1 = (x == 1) | (x == 2)
    relays_3 = (t == 5) | (t == 6) | ((x == 3) & ~first)

    cp = {
        S1: (x != 3, lambda c: copy(own(c), hal.at[0, c], S1, c, down(1), place)),
        S3: ((t == 0) | ((t == 1) & first) | (t == 2) | (t == 4), lambda c: copy(own(c), hal.at[2, c], S3, c, down(3), place)),
        R2: (relays_1 & first, lambda c: copy(hal.at[0, c], hal.at[1, c], R2, c, down(1), place)),
        X2: (relays_3, lambda c: copy(hal.at[2, c], hal.at[1, c], X2, c, down(tsize - 1), place, R2)),
        Y3: (t == 3, lambda c: copy(own(c), in3.at[c], Y3, c, down(4), place)),
        P0: (((t == 1) | (t == 5)) & ~first, lambda c: copy(own(c), in2.at[c], P0, c, down(tsize - 1), place)),
        P2: ((x == 0) & ~first, lambda c: copy(in2.at[c], hal.at[1, c], P2, c, down(3), place, R2)),
        P4: ((t == 0) & ~first, lambda c: copy(in2.at[c], hal.at[2, c], P4, c, down(4), place, S3)),
        Z1: (t == 7, lambda c: copy(in3.at[c], hal.at[0, c], Z1, c, down(tsize - 3), place, S1)),
        Z3: (t == 7, lambda c: copy(in3.at[c], hal.at[2, c], Z3, c, down(tsize - 1), place, S3)),
        SA: (None, lambda c: copy(part.at[c, row((1 - core) * half, half)], got_a.at[c], SA, c, t, other_core)),
        SB: (y_first, lambda c: copy(part.at[c, row(theirs_y, quarter)], got_b.at[c], SB, c, t, other_y)),
        TB: (~y_first, lambda c: copy(part.at[c, row(over_y, piece)], got_b.at[c, 0:piece], TB, c, t, other_y, SB)),
        GB: (y_first, lambda c: copy(full.at[c, row(mine_y, quarter)], full.at[c, row(mine_y, quarter)], GB, c, t, other_y)),
        HB: (~y_first, lambda c: copy(full.at[c, row(mine, piece)], full.at[c, row(mine, piece)], HB, c, t, other_y, GB)),
        GA: (None, lambda c: copy(full.at[c, row(core * half, half)], full.at[c, row(core * half, half)], GA, c, t, other_core)),
        D2: ((x >= 2) & first, lambda c: copy(adj.at[1, c], in2.at[c], D2, c, down(tsize - 1), place)),
        D1: (x >= 1, lambda c: copy(adj.at[0, c], in1.at[c], D1, c, down(tsize - 1), place)),
        D3: (x == 3, lambda c: copy(adj.at[2, c], in3.at[c], D3, c, down(tsize - 3), place)),
        F1: (t == 7, lambda c: copy(in_a.at[c], in3.at[c], F1, c, down(tsize - 4), place, D3)),
        V3: (((t == 4) & first) | (t == 5), lambda c: copy(adj.at[2, c], in_a.at[c], V3, c, down(tsize - 4), other_y)),
        G2: ((x == 2) & ~first, lambda c: copy(adj.at[1, c], in2.at[c], G2, c, down(1), place, D2)),
        G3: ((x == 3) & ~first, lambda c: copy(adj.at[1, c], in_b.at[c], G3, c, down(tsize - 3), place, E2)),
        V1: ((t == 4) & ~first, lambda c: copy(adj.at[2, c], in_a.at[c], V1, c, down(tsize - 4), place, V3)),
        W1: ((t == 0) & ~first, lambda c: copy(in_a.at[c], in3.at[c], W1, c, down(1), place, D3)),
        U1: ((t == 4) & ~first, lambda c: copy(in_b.at[c], in3.at[c], U1, c, down(1), place, D3)),
        W3: (((t == 0) & first) | (t == 1), lambda c: copy(in_a.at[c], in3.at[c], W3, c, down(1), other_y, D3)),
        E1: ((t == 5) | (t == 6), lambda c: copy(adj.at[t - 4, c], in_a.at[c], E1, c, down(1), place)),
        E2: (t == 4, lambda c: copy(adj.at[1, c], in_b.at[c], E2, c, down(1), place)),
        E3: (t == 4, lambda c: copy(adj.at[0, c], in_b.at[c], E3, c, down(3), place, E2)),
    }

    def c_send(step, c, size, base):
        to = lax.rem(z + step, nz)
        return copy(part.at[c, row(base + to * size, size)], got_c.at[c, step - 1, 0:size], SC + step - 1, c, t, z_peer(step))

    def c_gather(step, c, size, base):
        at = row(base + z * size, size)
        return copy(full.at[c, at], full.at[c, at], SC + gz + step - 1, c, t, z_peer(step))

    def start(kind, c, when=None):
        cond = cp[kind][0] if when is None else when
        if cond is None or cond is True:
            cp[kind][1](c).start()
        else:
            pl.when(cond)(lambda: cp[kind][1](c).start())

    def landed(ref, kind, c, when=None):
        def wait():
            copy(ref, ref, kind, c, t, other_core).wait_recv()

        if when is None:
            wait()
        else:
            pl.when(when)(wait)

    def own_sends(c):
        start(Y3, c)
        start(P0, c)
        start(S3, c)
        start(S1, c)

    def relay_1(c):
        @pl.when(t == 7)
        def _():
            landed(in3.at[c], Y3, c)
            start(Z1, c, True)
            start(Z3, c, True)

        @pl.when((x == 0) & ~first)
        def _():
            landed(in2.at[c], P0, c)
            start(P2, c, True)
            start(P4, c, t == 0)

        early = relays_3 & (t != 6)
        landed(hal.at[2, c], H3, c, early)
        start(X2, c, early)
        landed(hal.at[0, c], H1, c, relays_1 & first)
        start(R2, c)

    def relay_2(c):
        landed(hal.at[2, c], H3, c, t == 6)
        start(X2, c, t == 6)

    def forward(c):
        landed(hal.at[0, c], H1, c, (t >= 1) & ~(relays_1 & first))
        landed(hal.at[1, c], H2, c, t >= 2)
        landed(hal.at[2, c], H3, c, (t >= 3) & ~relays_3)
        for lag in range(LAGS):
            value = flux[:, cols(c)] if lag == 0 else hal[lag - 1, c]
            high, low = split(value)
            f_hi[lag * deep : (lag + 1) * deep, :] = high
            f_lo[lag * deep : (lag + 1) * deep, :] = low

        tile = rows // 4

        def block(m, carry):
            at = pl.ds(pl.multiple_of(m * tile, 8), tile)
            hh, hl = h_hi[at, :], h_lo[at, :]
            total = jnp.dot(hh, f_hi[...], preferred_element_type=jnp.float32)
            total = total + jnp.dot(hh, f_lo[...], preferred_element_type=jnp.float32)
            total = total + jnp.dot(hl, f_hi[...], preferred_element_type=jnp.float32)
            part[c, at, :] = total
            return carry

        lax.fori_loop(0, 4, block, 0)
        start(SA, c)

    def spread(c, size, base):
        for step in range(1, nz):
            c_send(step, c, size, base).start()

    def collect(c, size, base):
        at = row(base + z * size, size)
        total = part[c, at, :]
        for step in range(1, nz):
            landed(got_c.at[c, step - 1, 0:size], SC + step - 1, c)
            total = total + got_c[c, step - 1, 0:size, :]
        return at, total

    def share(c, size, base):
        for step in range(1, nz):
            c_gather(step, c, size, base).start()

    def shared(c, size, base):
        for step in range(1, nz):
            landed(full.at[c, row(base + z_from(step) * size, size)], SC + gz + step - 1, c)

    def sum_1(c):
        landed(got_a.at[c], SA, c)
        at = row(top, half)
        part[c, at, :] = part[c, at, :] + got_a[c]
        start(SB, c)
        pl.when(~y_first)(lambda: spread(c, pair, top))

    def sum_2(c):
        @pl.when(y_first)
        def _():
            landed(got_b.at[c], SB, c)
            at = row(mine_y, quarter)
            part[c, at, :] = part[c, at, :] + got_b[c]
            spread(c, piece, mine_y)

        @pl.when(~y_first)
        def _():
            at, total = collect(c, pair, top)
            part[c, at, :] = total
            start(TB, c, True)

    def sum_3(c):
        @pl.when(y_first)
        def _():
            at, total = collect(c, piece, mine_y)
            full[c, at, :] = total * scale[:, 0:1]
            share(c, piece, mine_y)

        @pl.when(~y_first)
        def _():
            landed(got_b.at[c, 0:piece], SB, c)
            at = row(mine, piece)
            full[c, at, :] = (part[c, at, :] + got_b[c, 0:piece]) * scale[:, 0:1]
            start(HB, c, True)

    def gather_1(c):
        @pl.when(y_first)
        def _():
            shared(c, piece, mine_y)
            start(GB, c, True)

        @pl.when(~y_first)
        def _():
            landed(full.at[c, row(over_y, piece)], GB, c)
            share(c, pair, top)

    def gather_2(c):
        landed(full.at[c, row(theirs_y, quarter)], GB, c, y_first)
        pl.when(~y_first)(lambda: shared(c, pair, top))
        start(GA, c)

    def adjoint(c):
        landed(full.at[c, row((1 - core) * half, half)], GA, c)
        high, low = split(full[c])
        w_hi[...] = high
        w_lo[...] = low

        def block(lag):
            at = pl.ds(lag * deep, deep)
            hh, hl = t_hi[at, :], t_lo[at, :]
            total = jnp.dot(hh, w_hi[...], preferred_element_type=jnp.float32)
            total = total + jnp.dot(hh, w_lo[...], preferred_element_type=jnp.float32)
            return total + jnp.dot(hl, w_hi[...], preferred_element_type=jnp.float32)

        adj[2, c] = block(3)
        adj[1, c] = block(2)
        start(D2, c)
        start(G2, c)
        start(G3, c)
        start(E2, c)
        start(E1, c, t == 5)
        start(D3, c, (x == 3) & first)
        start(V3, c, (t == 4) & first)
        start(V1, c)
        adj[0, c] = block(1)
        start(E3, c)
        start(D1, c, (x == 3) | ((x >= 1) & ~first))
        out[:, cols(c)] = block(0)

    def back_1(c):
        @pl.when(t == 6)
        def _():
            landed(in_a.at[c], E1, c)
            adj[2, c] = adj[2, c] + in_a[c]
            start(E1, c, True)

        @pl.when(t == 5)
        def _():
            landed(in_b.at[c], E2, c)
            adj[2, c] = adj[2, c] + in_b[c]
            start(V3, c, True)

        @pl.when(relays_1 & first)
        def _():
            landed(in2.at[c], D2, c)
            adj[0, c] = adj[0, c] + in2[c]
            start(D1, c, True)

        @pl.when((x == 3) & ~first)
        def _():
            landed(in2.at[c], D2, c)
            adj[2, c] = adj[2, c] + in2[c]
            start(D3, c, True)

        @pl.when((t == 0) & ~first)
        def _():
            landed(in_a.at[c], V3, c)
            landed(in_b.at[c], E2, c)
            in_a[c] = in_a[c] + in_b[c]
            start(W1, c, True)

        @pl.when((t == 4) & ~first)
        def _():
            landed(in_b.at[c], E2, c)
            start(U1, c, True)

    def back_2(c):
        @pl.when(t == 7)
        def _():
            landed(in_b.at[c], E2, c)
            landed(in_a.at[c], E1, c)
            in_a[c] = in_a[c] + in_b[c]
            start(F1, c, True)

    def cross_1(c):
        landed(in_a.at[c], V3, c, cp[W3][0])
        start(W3, c)

    def finish(c):
        @pl.when(x <= 2)
        def _():
            landed(in1.at[c], D1, c)
            out[:, cols(c)] = out[:, cols(c)] + in1[c]

        @pl.when((t <= 4) | ((t == 5) & ~first))
        def _():
            landed(in3.at[c], D3, c)
            out[:, cols(c)] = out[:, cols(c)] + in3[c]

    def split_rows(lag):
        at = pl.ds(lag * deep, deep)
        h_hi[:, at], h_lo[:, at] = split(foot[lag])

    def split_turned(lag):
        at = pl.ds(lag * deep, deep)
        t_hi[at, :], t_lo[at, :] = split(foot[lag].T)

    def late_sends(c):
        pl.when(c >= LEAD)(lambda: own_sends(c))

    for c in range(LEAD):
        own_sends(c)
    with jax.named_scope('p_split'):
        split_rows(0)
        split_rows(1)
    with jax.named_scope('p_relay'):
        relay_1(0)
    with jax.named_scope('p_split'):
        split_rows(2)
        split_rows(3)
    for lag in range(1, LAGS):

        @pl.when(t < lag)
        def _(lag=lag):
            hal[lag - 1] = jnp.zeros(hal.shape[1:], hal.dtype)

    def late_relay(c):
        pl.when(c >= 1)(lambda: relay_1(c))

    def turn(c):
        @pl.when(c == 0)
        def _():
            for lag in range(LAGS):
                split_turned(lag)

    named = locals()
    order = [(named[name], delay) for name, delay in ORDER]
    begin, end = min(d for _, d in order), max(d for _, d in order)

    def step(i, carry):
        for stage, delay in order:
            c = i - delay
            @pl.when((c >= 0) & (c < chunks))
            def _(stage=stage, c=c):
                with jax.named_scope(stage.__name__):
                    stage(c)
        return carry

    lax.fori_loop(begin, chunks + end, step, 0)

    def drain(c, carry):
        for kind, (cond, make) in cp.items():
            if cond is None:
                make(c).wait_send()
            else:
                pl.when(cond)(lambda make=make: make(c).wait_send())
        for cond, size, base in sides:

            @pl.when(cond)
            def _(size=size, base=base):
                for s in range(1, nz):
                    c_send(s, c, size, base).wait_send()
                    c_gather(s, c, size, base).wait_send()

        return carry

    lax.fori_loop(0, chunks, drain, 0)


def on_device(footprint, flux, obs_weight, obs_count):
    lags, slots, deep = footprint.shape[1:]
    wide = flux.shape[2]
    chunks = CHUNKS
    width = wide // chunks
    nz = lax.axis_size("cells") // 4
    piece = slots // (4 * nz)
    place = lax.axis_index("cells")
    core, y, z = lax.rem(place, 2), lax.rem(place // 2, 2), place // 4
    inner = jnp.where(core == 0, y * (slots // 4) + z * piece, (2 * z + y) * piece)
    base = core * (slots // 2) + inner
    mine = base + jnp.arange(piece, dtype=jnp.int32)
    weight = lax.dynamic_slice(obs_weight[0], (base,), (piece,))
    row_scale = jnp.where(mine < obs_count[0], weight, 0.0)
    scale = jnp.broadcast_to(row_scale[:, None], (piece, 128))
    f32, bf16 = jnp.float32, jnp.bfloat16
    wide_block = pltpu.VMEM((chunks, deep, width), f32)
    kinds = SC + 2 * (nz - 1)
    result = pl.pallas_call(
        kernel,
        out_shape=jax.ShapeDtypeStruct((deep, wide), f32),
        in_specs=[pl.BlockSpec(memory_space=pltpu.VMEM)] * 3,
        out_specs=pl.BlockSpec(memory_space=pltpu.VMEM),
        scratch_shapes=[
            pltpu.VMEM((lags - 1, chunks, deep, width), f32),
            pltpu.VMEM((chunks, slots, width), f32),
            pltpu.VMEM((chunks, slots // 2, width), f32),
            pltpu.VMEM((chunks, slots // 4, width), f32),
            pltpu.VMEM((chunks, nz - 1, 2 * piece, width), f32),
            pltpu.VMEM((chunks, slots, width), f32),
            pltpu.VMEM((lags - 1, chunks, deep, width), f32),
            wide_block,
            wide_block,
            wide_block,
            wide_block,
            wide_block,
            pltpu.VMEM((slots, lags * deep), bf16),
            pltpu.VMEM((slots, lags * deep), bf16),
            pltpu.VMEM((lags * deep, slots), bf16),
            pltpu.VMEM((lags * deep, slots), bf16),
            pltpu.VMEM((lags * deep, width), bf16),
            pltpu.VMEM((lags * deep, width), bf16),
            pltpu.VMEM((slots, width), bf16),
            pltpu.VMEM((slots, width), bf16),
            pltpu.SemaphoreType.DMA((kinds, chunks)),
            pltpu.SemaphoreType.DMA((kinds, chunks)),
        ],
        compiler_params=pltpu.CompilerParams(
            collective_id=0, has_side_effects=True, vmem_limit_bytes=67043328
        ),
    )(footprint[0], flux[0], scale)
    return result[None]


def solution(mesh):
    placed = (P("tm", None, None, "cells"), P("tm", "cells", None), P("tm", None), P("tm"))
    return jax.shard_map(
        on_device, mesh=mesh, in_specs=placed, out_specs=P("tm", "cells", None), check_vma=False
    )
```
